32 devices in a mesh: node: 32 (over z, y, x, core).
Axes of the slice: x: 2, y: 2, z: 4, core: 2. Of those that a mesh axis runs over, the one named last changes fastest.
Arguments:
- event_node: int32 [16384], P('node'), may hold values from 0 to 8191, as said below
- neighbours: int32 [16384, 10], P('node'), may hold values from 0 to 8191, as said below
- event_bucket: int32 [16384], P('node'), may hold values from 0 to 127
- neighbour_bucket: int32 [16384, 10], P('node'), may hold values from 0 to 127
- edge_features: bfloat16 [16384, 128], P('node'), may hold values from -6 to 6
- affinity: float32 [16384, 10], P('node'), may hold values from -320 to 320
- upstream: bfloat16 [16384, 512], P('node'), may hold values from -6 to 6
- node_memory: bfloat16 [8192, 512], P('node'), may hold values from -4 to 4
- edge_weight: bfloat16 [128, 512], replicated, may hold values from -0.5 to 0.5
- time_message: float32 [128, 512], replicated, may hold values from -6 to 6
- input_weight: bfloat16 [512, 1536], replicated, may hold values from -0.25 to 0.25
- hidden_weight: bfloat16 [512, 1536], replicated, may hold values from -0.25 to 0.25
- gate_bias: float32 [1536], replicated, may hold values from -6 to 6
- time_key: float32 [128, 512], replicated, may hold values from -6 to 6
- query_weight: bfloat16 [512, 512], replicated, may hold values from -0.25 to 0.25
- key_weight: bfloat16 [512, 512], replicated, may hold values from -0.25 to 0.25
- value_weight: bfloat16 [512, 512], replicated, may hold values from -0.25 to 0.25
- out_weight: bfloat16 [512, 512], replicated, may hold values from -0.25 to 0.25
Outputs:
- embedding: bfloat16 [16384, 512], P('node')
- new_memory: bfloat16 [8192, 512], P('node')
- grad_query: float32 [512, 512], replicated
- grad_key: float32 [512, 512], replicated
- grad_value: float32 [512, 512], replicated
- grad_out: float32 [512, 512], replicated
The draws below stay inside these ranges and needn't reach their ends.
Inputs may be any that keep to these rules, and one draw needn't show every extreme that they name: `event_node`: node i belongs to index i // 256 of node. Of the 512 rows of one device, at most 48 name nodes of one index; in every draw one index receives exactly 48 of them from every device. `neighbours`: node i belongs to index i // 256 of node. Of the 5120 entries of one device's rows, at most 320 name nodes of one index, and these name at most 64 distinct nodes; in every draw one index receives exactly 320 entries naming exactly 64 distinct nodes from every device.
All inputs are finite; a program needn't handle non-finite values.
Results may differ from the reference program's by a relative error of at most 0.012.
Values may be sent and summed in bfloat16 or wider, within the bound.
A program may use at most 192 MiB of HBM per device.

```python
import math
import jax
import jax.numpy as jnp
from jax import lax

MEM = 512
MSG = 512
EDGE = 128
HEADS = 2
NEIGH = 10
TBUCK = 128
CAPU = 64
EV_DEV = 512
NODE_DEV = 256
EVENTS = 16384
NODES = 8192
CAPM = 48
CAPN = 320
N_NODE = 32


def packed_owners(device_key, amount, capacity, hottest):
    slots_all = N_NODE * capacity
    slot_ids = jnp.arange(slots_all, dtype=jnp.int32)
    owners = slot_ids // capacity
    within = slot_ids % capacity
    priority = jax.random.permutation(jax.random.fold_in(device_key, 1), slots_all).astype(jnp.int32) + 1
    priority = jnp.where(owners == hottest, 0, priority)
    ordered = jnp.argsort(priority, stable=True)[:amount]
    shuffled = ordered[jax.random.permutation(jax.random.fold_in(device_key, 2), amount)]
    return (owners[shuffled], within[shuffled])


def draw_event_node(key, part):
    hottest = jax.random.randint(jax.random.fold_in(key, 11), (), 0, N_NODE)

    def device(number):
        device_key = jax.random.fold_in(jax.random.fold_in(key, 12), number)
        owners, within = packed_owners(device_key, EV_DEV, CAPM, hottest)
        local_rows = jax.random.randint(jax.random.fold_in(device_key, 3), (EV_DEV,), 0, NODE_DEV)
        return owners * NODE_DEV + local_rows
    return jax.vmap(device)(jnp.arange(N_NODE, dtype=jnp.int32)).reshape(-1).astype(jnp.int32)


def draw_neighbours(key, part):
    hottest = jax.random.randint(jax.random.fold_in(key, 21), (), 0, N_NODE)

    def device(number):
        device_key = jax.random.fold_in(jax.random.fold_in(key, 22), number)
        owners, within = packed_owners(device_key, EV_DEV * NEIGH, CAPN, hottest)

        def pool_of(owner_id):
            return jax.random.permutation(jax.random.fold_in(device_key, 1000 + owner_id), NODE_DEV)[:CAPU]
        pools = jax.vmap(pool_of)(jnp.arange(N_NODE, dtype=jnp.int32))
        local_rows = pools[owners, within % CAPU]
        return (owners * NODE_DEV + local_rows).reshape(EV_DEV, NEIGH)
    whole = jax.vmap(device)(jnp.arange(N_NODE, dtype=jnp.int32))
    return whole.reshape(EV_DEV * N_NODE, NEIGH).astype(jnp.int32)


def draw_affinity(key, part):
    rows_all = EV_DEV * N_NODE
    return jax.random.normal(jax.random.fold_in(key, 1), (rows_all, NEIGH), jnp.float32)


def touch_ends(entries, stream_key, smallest, high):
    spot = [jax.random.randint(jax.random.fold_in(stream_key, axis), (), 0, length) for axis, length in enumerate(entries.shape)]
    longest = entries.shape.index(max(entries.shape))
    beside = spot[:longest] + [(spot[longest] + 1) % entries.shape[longest]] + spot[longest + 1:]
    return entries.at[tuple(spot)].set(smallest).at[tuple(beside)].set(high)


def block_scale(rng, shape, split, least, high):
    level, own = 1.0, jax.random.fold_in(rng, 6)
    for dim, shards_of in split:
        draws = jnp.exp(jax.random.uniform(jax.random.fold_in(own, dim), (shards_of,), jnp.float32, least / len(split), high / len(split)))
        level = level * jnp.repeat(draws, shape[dim] // shards_of).reshape([-1 if axis == dim else 1 for axis in range(len(shape))])
    return level


def scatter_about(rng, extent, width, reach, shards=(), kind=jnp.bfloat16):
    drawn = jax.random.normal(rng, extent, jnp.float32) * width
    if len(shards) > 0:
        drawn = block_scale(rng, extent, shards, -0.22, 0.18) * drawn
    return jnp.clip(drawn, min=-reach, max=reach).astype(kind)


def setup_inputs(seed: int = 0) -> dict:
    seeds = jax.random.split(jax.random.key(seed), 19)
    event_node = draw_event_node(jax.random.fold_in(seeds[18], 71), 0)
    neighbours = draw_neighbours(jax.random.fold_in(seeds[18], 71), 0)
    event_bucket = touch_ends(jax.random.randint(seeds[2], (EVENTS,), 0, TBUCK), jax.random.fold_in(seeds[2], 1), 0, TBUCK - 1).astype(jnp.int32)
    neighbour_bucket = touch_ends(jax.random.randint(seeds[3], (EVENTS, NEIGH), 0, TBUCK), jax.random.fold_in(seeds[3], 1), 0, TBUCK - 1).astype(jnp.int32)
    edge_features = scatter_about(seeds[4], (EVENTS, EDGE), 1.0, 6.0, ((0, 32),))
    affinity = draw_affinity(jax.random.fold_in(seeds[18], 71), 0)
    upstream = scatter_about(seeds[6], (EVENTS, MEM), 1.0, 6.0, ((0, 32),))
    node_memory = scatter_about(seeds[7], (NODES, MEM), 1.0, 4.0, ((0, 32),))
    edge_weight = scatter_about(seeds[8], (EDGE, MSG), EDGE ** -0.5, 0.5)
    time_message = scatter_about(seeds[9], (TBUCK, MSG), 1.0, 6.0, (), jnp.float32)
    input_weight = scatter_about(seeds[10], (MSG, 3 * MEM), MSG ** -0.5, 0.25)
    hidden_weight = scatter_about(seeds[11], (MEM, 3 * MEM), MEM ** -0.5, 0.25)
    gate_bias = scatter_about(seeds[12], (3 * MEM,), 1.0, 6.0, (), jnp.float32)
    time_key = scatter_about(seeds[13], (TBUCK, MEM), 1.0, 6.0, (), jnp.float32)
    query_weight = scatter_about(seeds[14], (MEM, MEM), MEM ** -0.5, 0.25)
    key_weight = scatter_about(seeds[15], (MEM, MEM), MEM ** -0.5, 0.25)
    value_weight = scatter_about(seeds[16], (MEM, MEM), MEM ** -0.5, 0.25)
    out_weight = scatter_about(seeds[17], (MEM, MEM), MEM ** -0.5, 0.25)
    return {"event_node": event_node, "neighbours": neighbours, "event_bucket": event_bucket, "neighbour_bucket": neighbour_bucket, "edge_features": edge_features, "affinity": affinity, "upstream": upstream, "node_memory": node_memory, "edge_weight": edge_weight, "time_message": time_message, "input_weight": input_weight, "hidden_weight": hidden_weight, "gate_bias": gate_bias, "time_key": time_key, "query_weight": query_weight, "key_weight": key_weight, "value_weight": value_weight, "out_weight": out_weight}


def make_message(edge_rows, buckets, edge_weight, time_message):
    before = jnp.dot(edge_rows, edge_weight, preferred_element_type=jnp.float32) + jnp.take(time_message, buckets, axis=0)
    return jax.nn.silu(before).astype(jnp.bfloat16)

def gru_rows(aggregate, previous, input_weight, hidden_weight, gate_bias):
    columns = previous.shape[1]
    inputs = jnp.dot(aggregate, input_weight, preferred_element_type=jnp.float32) + gate_bias
    hidden = jnp.dot(previous, hidden_weight, preferred_element_type=jnp.float32)
    update = jax.nn.sigmoid(inputs[:, :columns] + hidden[:, :columns])
    resets = jax.nn.sigmoid(inputs[:, columns:2 * columns] + hidden[:, columns:2 * columns])
    candidate = jnp.tanh(inputs[:, 2 * columns:] + resets * hidden[:, 2 * columns:])
    return (1.0 - update) * candidate + update * previous.astype(jnp.float32)

def attend(target, neighbour_rows, neighbour_bucket, affinity, time_key, query_weight, key_weight, value_weight, out_weight):
    events, fanout, columns = neighbour_rows.shape
    head_size = columns // HEADS
    query = jnp.dot(target, query_weight, preferred_element_type=jnp.float32).astype(jnp.bfloat16).reshape(events, HEADS, head_size)
    flat_rows = neighbour_rows.reshape(events * fanout, columns)
    key_rows = jnp.dot(flat_rows, key_weight, preferred_element_type=jnp.float32) + jnp.take(time_key, neighbour_bucket.reshape(-1), axis=0)
    key_rows = key_rows.astype(jnp.bfloat16).reshape(events, fanout, HEADS, head_size)
    value_rows = jnp.dot(flat_rows, value_weight, preferred_element_type=jnp.float32).astype(jnp.bfloat16).reshape(events, fanout, HEADS, head_size)
    scores = jnp.einsum('ehd,enhd->ehn', query.astype(jnp.float32), key_rows.astype(jnp.float32)) / math.sqrt(head_size)
    scores = scores + affinity[:, None, :]
    probs = jax.nn.softmax(scores, axis=-1).astype(jnp.bfloat16)
    mixed = jnp.einsum('ehn,enhd->ehd', probs.astype(jnp.float32), value_rows.astype(jnp.float32))
    mixed = mixed.astype(jnp.bfloat16).reshape(events, columns)
    return (jnp.dot(mixed, out_weight, preferred_element_type=jnp.float32) + target.astype(jnp.float32)).astype(jnp.bfloat16)

def reference(event_node, neighbours, event_bucket, neighbour_bucket, edge_features, affinity, upstream, node_memory, edge_weight, time_message, input_weight, hidden_weight, gate_bias, time_key, query_weight, key_weight, value_weight, out_weight):
    messages = make_message(edge_features, event_bucket, edge_weight, time_message)
    totals = jax.ops.segment_sum(messages.astype(jnp.float32), event_node, num_segments=NODES)
    counts = jax.ops.segment_sum(jnp.ones(event_node.shape, jnp.float32), event_node, num_segments=NODES)
    aggregate = (totals / jnp.maximum(counts, 1.0)[:, None]).astype(jnp.bfloat16)
    updated = gru_rows(aggregate, node_memory, input_weight, hidden_weight, gate_bias)
    new_memory = jnp.where(counts[:, None] > 0, updated, node_memory.astype(jnp.float32)).astype(jnp.bfloat16)

    def block(carry, number):
        start = number * EV_DEV
        targets = lax.dynamic_slice_in_dim(event_node, start, EV_DEV)
        nearby = lax.dynamic_slice_in_dim(neighbours, start, EV_DEV)
        buckets = lax.dynamic_slice_in_dim(neighbour_bucket, start, EV_DEV)
        logits = lax.dynamic_slice_in_dim(affinity, start, EV_DEV)
        tangent = lax.dynamic_slice_in_dim(upstream, start, EV_DEV)
        target_rows = jnp.take(new_memory, targets, axis=0)
        nearby_rows = jnp.take(new_memory, nearby.reshape(-1), axis=0).reshape(EV_DEV, NEIGH, MEM)

        def forward(weight_q, weight_k, weight_v, weight_o):
            return attend(target_rows, nearby_rows, buckets, logits, time_key, weight_q, weight_k, weight_v, weight_o)
        result, pullback = jax.vjp(forward, query_weight, key_weight, value_weight, out_weight)
        grads = pullback(tangent)
        carry = tuple((total + grad.astype(jnp.float32) for total, grad in zip(carry, grads)))
        return (carry, result)
    zeros_start = tuple((jnp.zeros((MEM, MEM), jnp.float32) for _ in range(4)))
    summed, blocks = lax.scan(block, zeros_start, jnp.arange(N_NODE, dtype=jnp.int32))
    embedding = blocks.reshape(EVENTS, MEM)
    factor = 1.0 / math.sqrt(EVENTS)
    return (embedding, new_memory, summed[0] * factor, summed[1] * factor, summed[2] * factor, summed[3] * factor)
```

```python
import functools
import math

import jax
import jax.numpy as jnp
from jax import lax
from jax.experimental import pallas as pl
from jax.experimental.pallas import tpu as pltpu
from jax.sharding import PartitionSpec as P

HEADS = 2
LANES = 128
GROUP = 32
BF = jnp.bfloat16
F32 = jnp.float32
VMEM_LIMIT = 60 * 1024 * 1024
RESIDENT_LIMIT = 20 * 1024 * 1024
NT = (((1,), (1,)), ((), ()))
TN = (((0,), (0,)), ((), ()))


def mm(a, b):
    return jnp.dot(a, b, preferred_element_type=F32)


def mm_nt(a, b):
    return lax.dot_general(a, b, NT, preferred_element_type=F32)


def mm_tn(a, b):
    return lax.dot_general(a, b, TN, preferred_element_type=F32)


def halves(table):
    high = table.astype(BF)
    low = (table - high.astype(F32)).astype(BF)
    return high, low


def memory_kernel(
    devices,
    events,
    slots,
    chunk,
    feats,
    meta,
    owners,
    memory,
    edge_weight,
    time_message,
    input_weight,
    hidden_weight,
    gate_bias,
    out_memory,
    out_table,
    sel,
    picked,
    picked_meta,
    totals,
    counts,
    wide,
):
    me = lax.axis_index("node")
    rows = memory.shape[0]
    columns = memory.shape[1]
    stride = columns // LANES
    mine = owners[...] == me.astype(F32)
    before = lax.broadcasted_iota(jnp.int32, (events, events), 0) < lax.broadcasted_iota(
        jnp.int32, (events, events), 1
    )
    rank = mm(mine.astype(F32).astype(BF), before.astype(F32).astype(BF))
    sel[...] = jnp.where(mine, rank, -1.0)
    slot_ids = lax.broadcasted_iota(jnp.int32, (slots, events), 0).astype(F32)

    def pick(step, carry):
        for half in range(4):
            source = step * 4 + half
            hits = (slot_ids == sel[pl.ds(source, 1), :]).astype(F32).astype(BF)
            at = pl.ds(pl.multiple_of(source * slots, slots), slots)
            picked[at, :] = mm(hits, feats[source, :events, :]).astype(BF)
            picked_meta[at, :] = mm_nt(hits, meta[source])
        return carry

    lax.fori_loop(0, devices // 4, pick, 0)
    totals[...] = jnp.zeros_like(totals)
    counts[...] = jnp.zeros_like(counts)
    high, low = halves(time_message[...])
    weight = edge_weight[...]

    def add(step, carry):
        at = pl.ds(pl.multiple_of(step * chunk, chunk), chunk)
        info = picked_meta[at, :]
        node, bucket, valid = info[:, 0:1], info[:, 1:2], info[:, 2:3]
        lanes = lax.broadcasted_iota(jnp.int32, (chunk, high.shape[0]), 1).astype(F32)
        picks = (lanes == bucket).astype(F32).astype(BF)
        pre = mm(picked[at, :], weight) + mm(picks, high) + mm(picks, low)
        message = (pre / (1.0 + jnp.exp(-pre))).astype(BF)
        ids = lax.broadcasted_iota(jnp.int32, (chunk, rows), 1).astype(F32)
        hot = jnp.where(ids == node, valid, 0.0).astype(BF)
        totals[...] += mm_tn(hot, message)
        counts[...] += mm_tn(hot, jnp.ones((chunk, LANES), BF))
        return carry

    lax.fori_loop(0, devices * slots // chunk, add, 0)
    count = counts[:, 0:1]
    aggregate = (totals[...] / jnp.maximum(count, 1.0)).astype(BF)
    previous = memory[...]

    def gate(which):
        cut = slice(which * columns, (which + 1) * columns)
        return (
            mm(aggregate, input_weight[:, cut]) + gate_bias[:, cut],
            mm(previous, hidden_weight[:, cut]),
        )

    from_input, from_hidden = gate(0)
    update = jax.nn.sigmoid(from_input + from_hidden)
    from_input, from_hidden = gate(1)
    resets = jax.nn.sigmoid(from_input + from_hidden)
    from_input, from_hidden = gate(2)
    candidate = jnp.tanh(from_input + resets * from_hidden)
    old = previous.astype(F32)
    fresh = (1.0 - update) * candidate + update * old
    fresh = jnp.where(count > 0, fresh, old)
    out_memory[...] = fresh.astype(BF)
    for part in range(stride):
        wide[pl.ds(part, rows, stride=stride), :] = fresh[:, part * LANES : (part + 1) * LANES]
    out_table[...] = wide[...].astype(BF)


def event_kernel(
    resident,
    events,
    fanout,
    ids,
    source,
    buckets,
    affinity,
    upstream,
    time_key,
    query_weight,
    key_weight,
    value_weight,
    out_weight,
    embedding,
    grads,
    *scratch,
):
    columns = upstream.shape[1]
    head = columns // HEADS
    stride = columns // LANES
    if resident:
        landing, table, near, sems, *scratch = scratch
        parts = sems.shape[0]
        size = landing.shape[0] // parts
        copies = []
        for part in range(parts):
            at = pl.ds(part * size, size)
            copies.append(pltpu.make_async_copy(source.at[at], landing.at[at], sems.at[part]))
            copies[-1].start()
    else:
        near = source
        (*scratch,) = scratch
    target, query, back, pull, mix, hits, tq = scratch
    heads = [slice(h * head, (h + 1) * head) for h in range(HEADS)]
    high, low = halves(time_key[...])

    back[...] = mm_nt(upstream[...], out_weight[...]).astype(BF)
    for h, cut in enumerate(heads):
        pull[HEADS + h] = mm_nt(back[:, cut], value_weight[:, cut])

    if resident:
        step_rows = 256
        for part in range(parts):
            copies[part].wait()

            def widen(step, carry, part=part):
                at = pl.ds(pl.multiple_of(part * size + step * step_rows, step_rows), step_rows)
                table[at, :] = landing[at, :].astype(F32)
                return carry

            lax.fori_loop(0, size // step_rows, widen, 0)

        unroll = 16

        def fetch(step, carry):
            for lane in range(unroll):
                row = step * unroll + lane
                start = pl.multiple_of(ids[row], stride)
                near[pl.ds(pl.multiple_of(row * stride, stride), stride), :] = table[
                    pl.ds(start, stride), :
                ]
            return carry

        lax.fori_loop(0, (fanout + 1) * events // unroll, fetch, 0)

    for part in range(stride):
        target[:, part * LANES : (part + 1) * LANES] = near[
            pl.ds(fanout * events * stride + part, events, stride=stride), :
        ].astype(BF)
    query[...] = mm(target[...], query_weight[...]).astype(BF)
    for h, cut in enumerate(heads):
        pull[h] = mm_nt(query[:, cut], key_weight[:, cut])
        tq[h] = mm_nt(query[:, cut], high[:, cut]) + mm_nt(query[:, cut], low[:, cut])

    size = 32
    scale = 1.0 / math.sqrt(head)
    lane = lax.broadcasted_iota(jnp.int32, (size, LANES), 1)
    masks = [(lane >= h * GROUP) & (lane < h * GROUP + fanout) for h in range(HEADS)]

    def per_head(values, op, fill):
        out = jnp.zeros((size, LANES), F32)
        for mask in masks:
            out = jnp.where(
                mask, op(jnp.where(mask, values, fill), axis=1, keepdims=True), out
            )
        return out

    def block(step, carry):
        first = pl.multiple_of(step * size, size)
        at = pl.ds(first, size)
        names = buckets[at, :]

        def rows_of(j, part):
            return near[pl.ds((j * events + first) * stride + part, size, stride=stride), :]

        raw = jnp.zeros((size, LANES), F32)
        for j in range(fanout):
            same = lane == names[:, j : j + 1]
            nearby = [rows_of(j, part) for part in range(stride)]
            for k in range(2 * HEADS):
                total = nearby[0] * pull[k, at, 0:LANES]
                for part in range(1, stride):
                    total += nearby[part] * pull[k, at, part * LANES : (part + 1) * LANES]
                if k < HEADS:
                    total += jnp.where(same, tq[k, at, :], 0.0)
                raw = jnp.where(
                    lane == k * GROUP + j, jnp.sum(total, axis=1, keepdims=True), raw
                )
        scores = raw * scale + affinity[at, :]
        active = masks[0]
        for mask in masks[1:]:
            active = active | mask
        top = per_head(scores, jnp.max, -3.0e38)
        raised = jnp.where(active, jnp.exp(jnp.where(active, scores - top, 0.0)), 0.0)
        below = per_head(raised, jnp.sum, 0.0)
        probs = jnp.where(active, raised / jnp.where(active, below, 1.0), 0.0)
        turned = pltpu.roll(raw, HEADS * GROUP, axis=1).astype(BF).astype(F32)
        slopes = jnp.where(active, turned, 0.0)
        inner = per_head(probs * slopes, jnp.sum, 0.0)
        slopes = probs * (slopes - inner) * scale
        blend = jnp.where(
            active, probs.astype(BF).astype(F32), pltpu.roll(slopes, HEADS * GROUP, axis=1)
        )
        spread = [
            [
                jnp.broadcast_to(blend[:, k * GROUP + j : k * GROUP + j + 1], (size, LANES))
                for j in range(fanout)
            ]
            for k in range(2 * HEADS)
        ]
        for h in range(HEADS):
            total = jnp.zeros((size, LANES), F32)
            for j in range(fanout):
                total += jnp.where(lane == names[:, j : j + 1], spread[HEADS + h][j], 0.0)
            hits[h, at, :] = total.astype(BF)
        for part in range(stride):
            sums = [jnp.zeros((size, LANES), F32) for _ in range(2 * HEADS)]
            for j in range(fanout):
                nearby = rows_of(j, part)
                for k in range(2 * HEADS):
                    sums[k] += spread[k][j] * nearby
            for k in range(2 * HEADS):
                mix[k, at, part * LANES : (part + 1) * LANES] = sums[k].astype(BF)
        return carry

    lax.fori_loop(0, events // size, block, 0)

    for h, cut in enumerate(heads):
        grads[2 * columns : 3 * columns, cut] = mm_tn(mix[h], back[:, cut]).astype(BF)
        grads[columns : 2 * columns, cut] = mm_tn(mix[HEADS + h], query[:, cut]).astype(BF)
    for h, cut in enumerate(heads):
        back[:, cut] = mm(mix[h], value_weight[:, cut]).astype(BF)
        query[:, cut] = (
            mm(mix[HEADS + h], key_weight[:, cut])
            + mm(hits[h], high[:, cut])
            + mm(hits[h], low[:, cut])
        ).astype(BF)
    grads[:columns, :] = mm_tn(target[...], query[...]).astype(BF)
    grads[3 * columns :, :] = mm_tn(back[...], upstream[...]).astype(BF)
    embedding[...] = (mm(back[...], out_weight[...]) + target[...].astype(F32)).astype(BF)


def shards(
    event_node,
    neighbours,
    event_bucket,
    neighbour_bucket,
    edge_features,
    affinity,
    upstream,
    node_memory,
    edge_weight,
    time_message,
    input_weight,
    hidden_weight,
    gate_bias,
    time_key,
    query_weight,
    key_weight,
    value_weight,
    out_weight,
):
    devices = lax.axis_size("node")
    node_rows, columns = node_memory.shape
    events, fanout = neighbours.shape
    features = edge_features.shape[1]
    stride = columns // LANES
    slots = -(-(3 * events // devices) // 16) * 16
    vmem = pl.BlockSpec(memory_space=pltpu.VMEM)
    smem = pl.BlockSpec(memory_space=pltpu.SMEM)

    info_rows = events // features
    info = jnp.stack([event_node // node_rows, event_node % node_rows, event_bucket])
    info = info.astype(BF).reshape(3 * info_rows, features)
    tail = -(-3 * info_rows // 16) * 16
    packed = jnp.concatenate(
        [edge_features, info, jnp.zeros((tail - 3 * info_rows, features), BF)], axis=0
    )
    arrived = lax.all_gather(packed, "node", axis=0, tiled=False)
    numbers = arrived[:, events : events + 3 * info_rows, :].reshape(devices, 3, events)
    meta = jnp.concatenate(
        [
            numbers[:, 1:, :],
            jnp.ones((devices, 1, events), BF),
            jnp.zeros((devices, 5, events), BF),
        ],
        axis=1,
    )
    owners = numbers[:, 0, :].astype(F32)
    chunk = 256
    new_memory, own_table = pl.pallas_call(
        functools.partial(memory_kernel, devices, events, slots, chunk),
        out_shape=(
            jax.ShapeDtypeStruct((node_rows, columns), BF),
            jax.ShapeDtypeStruct((node_rows * stride, LANES), BF),
        ),
        in_specs=[vmem] * 9,
        out_specs=(vmem, vmem),
        scratch_shapes=[
            pltpu.VMEM((devices, events), F32),
            pltpu.VMEM((devices * slots, features), BF),
            pltpu.VMEM((devices * slots, 8), F32),
            pltpu.VMEM((node_rows, columns), F32),
            pltpu.VMEM((node_rows, LANES), F32),
            pltpu.VMEM((node_rows * stride, LANES), F32),
        ],
        compiler_params=pltpu.CompilerParams(vmem_limit_bytes=VMEM_LIMIT),
        name="memory_step",
    )(
        arrived,
        meta,
        owners,
        node_memory,
        edge_weight,
        time_message,
        input_weight,
        hidden_weight,
        gate_bias.reshape(1, -1),
    )
    whole = lax.all_gather(own_table, "node", axis=0, tiled=True)

    ids = jnp.concatenate([neighbours.T.reshape(-1), event_node]) * stride
    gap = jnp.zeros((events, GROUP - fanout), F32)
    rest = jnp.zeros((events, LANES - HEADS * GROUP), F32)
    logits = jnp.concatenate([affinity, gap] * HEADS + [rest], axis=1)
    buckets = jnp.pad(neighbour_bucket, ((0, 0), (0, LANES - fanout)))
    resident = whole.size * 4 <= RESIDENT_LIMIT
    near_rows = (fanout + 1) * events * stride
    if resident:
        source = whole
        source_spec = pl.BlockSpec(memory_space=pl.ANY)
        extra = [
            pltpu.VMEM(whole.shape, BF),
            pltpu.VMEM(whole.shape, F32),
            pltpu.VMEM((near_rows, LANES), F32),
            pltpu.SemaphoreType.DMA((8,)),
        ]
    else:
        source = whole.reshape(-1, stride, LANES)[ids // stride]
        source = source.reshape(near_rows, LANES).astype(F32)
        source_spec = vmem
        extra = []
    embedding, grads = pl.pallas_call(
        functools.partial(event_kernel, resident, events, fanout),
        out_shape=(
            jax.ShapeDtypeStruct((events, columns), BF),
            jax.ShapeDtypeStruct((4 * columns, columns), BF),
        ),
        in_specs=[smem, source_spec] + [vmem] * 8,
        out_specs=(vmem, vmem),
        scratch_shapes=extra
        + [
            pltpu.VMEM((events, columns), BF),
            pltpu.VMEM((events, columns), BF),
            pltpu.VMEM((events, columns), BF),
            pltpu.VMEM((2 * HEADS, events, columns), F32),
            pltpu.VMEM((2 * HEADS, events, columns), BF),
            pltpu.VMEM((HEADS, events, LANES), BF),
            pltpu.VMEM((HEADS, events, LANES), F32),
        ],
        compiler_params=pltpu.CompilerParams(vmem_limit_bytes=VMEM_LIMIT),
        name="event_step",
    )(
        ids,
        source,
        buckets,
        logits,
        upstream,
        time_key,
        query_weight,
        key_weight,
        value_weight,
        out_weight,
    )
    share = 4 * columns // devices
    factor = 1.0 / math.sqrt(events * devices)
    moved = lax.all_to_all(
        grads.reshape(devices, share, columns), "node", split_axis=0, concat_axis=0, tiled=True
    )
    summed = (jnp.sum(moved.astype(F32), axis=0) * factor).astype(BF)
    total = lax.all_gather(summed, "node", axis=0, tiled=True).astype(F32)
    return (embedding, new_memory) + tuple(
        total[part * columns : (part + 1) * columns] for part in range(4)
    )


def solution(mesh):
    placed = (
        P("node"),
        P("node", None),
        P("node"),
        P("node", None),
        P("node", None),
        P("node", None),
        P("node", None),
        P("node", None),
        P(),
        P(),
        P(),
        P(),
        P(),
        P(),
        P(),
        P(),
        P(),
        P(),
    )
    return jax.shard_map(
        shards,
        mesh=mesh,
        in_specs=placed,
        out_specs=(P("node", None), P("node", None), P(), P(), P(), P()),
        check_vma=False,
    )
```

```python
import functools
import math

import jax
import jax.numpy as jnp
from jax import lax
from jax.experimental import pallas as pl
from jax.experimental.pallas import tpu as pltpu
from jax.sharding import PartitionSpec as P

HEADS = 2
LANES = 128
GROUP = 32
BF = jnp.bfloat16
F32 = jnp.float32
VMEM_LIMIT = 60 * 1024 * 1024
RESIDENT_LIMIT = 20 * 1024 * 1024
NT = (((1,), (1,)), ((), ()))
TN = (((0,), (0,)), ((), ()))


def mm(a, b):
    return jnp.dot(a, b, preferred_element_type=F32)


def mm_nt(a, b):
    return lax.dot_general(a, b, NT, preferred_element_type=F32)


def mm_tn(a, b):
    return lax.dot_general(a, b, TN, preferred_element_type=F32)


def halves(table):
    high = table.astype(BF)
    low = (table - high.astype(F32)).astype(BF)
    return high, low


def pack_kernel(devices, slots, feats, meta, owners, outgoing, sel):
    events = feats.shape[0]
    ids = lax.broadcasted_iota(jnp.int32, (devices, events), 0)
    theirs = ids == owners[...]
    before = lax.broadcasted_iota(jnp.int32, (events, events), 0) < lax.broadcasted_iota(
        jnp.int32, (events, events), 1
    )
    rank = mm(theirs.astype(F32).astype(BF), before.astype(F32).astype(BF))
    sel[...] = jnp.where(theirs, rank, -1.0)
    slot_ids = lax.broadcasted_iota(jnp.int32, (slots, events), 0).astype(F32)
    lane_ids = lax.broadcasted_iota(jnp.int32, (LANES, events), 0).astype(F32)

    def pick(step, carry):
        for part in range(4):
            device = step * 4 + part
            row = sel[pl.ds(device, 1), :]
            hits = (slot_ids == row).astype(F32).astype(BF)
            outgoing[device, :slots, :] = mm(hits, feats[...]).astype(BF)
            turned = (lane_ids == row).astype(F32).astype(BF)
            outgoing[device, slots:, :] = mm_nt(meta[...], turned).astype(BF)
        return carry

    lax.fori_loop(0, devices // 4, pick, 0)


def exchange_kernel(devices, outgoing, inbox, send_sems, recv_sems, own_sem):
    me = lax.axis_index("node")
    barrier = pltpu.get_barrier_semaphore()

    def greet(step, carry):
        pl.semaphore_signal(
            barrier,
            inc=1,
            device_id=(lax.rem(me + step, devices),),
            device_id_type=pl.DeviceIdType.MESH,
        )
        return carry

    lax.fori_loop(1, devices, greet, 0)
    pl.semaphore_wait(barrier, devices - 1)

    def send(step):
        peer = lax.rem(me + step, devices)
        return pltpu.make_async_remote_copy(
            src_ref=outgoing.at[peer],
            dst_ref=inbox.at[me],
            send_sem=send_sems.at[peer],
            recv_sem=recv_sems.at[me],
            device_id=(peer,),
            device_id_type=pl.DeviceIdType.MESH,
        )

    def receive(step):
        peer = lax.rem(me + step, devices)
        return pltpu.make_async_remote_copy(
            src_ref=outgoing.at[peer],
            dst_ref=inbox.at[peer],
            send_sem=send_sems.at[peer],
            recv_sem=recv_sems.at[peer],
            device_id=(peer,),
            device_id_type=pl.DeviceIdType.MESH,
        )

    def start(step, carry):
        send(step).start()
        return carry

    def finish(step, carry):
        receive(step).wait_recv()
        send(step).wait_send()
        return carry

    lax.fori_loop(1, devices, start, 0)
    own = pltpu.make_async_copy(outgoing.at[me], inbox.at[me], own_sem)
    own.start()
    own.wait()
    lax.fori_loop(1, devices, finish, 0)


def reduce_kernel(
    chips,
    groups,
    factor,
    grads,
    result,
    near,
    pair,
    landed,
    share,
    pair_send,
    pair_recv,
    far_send,
    far_recv,
    back_send,
    back_recv,
    hop_send,
    hop_recv,
):
    me = lax.axis_index("node")
    core = lax.rem(me, 2)
    chip = me // 2
    partner = me + 1 - 2 * core
    half = grads.shape[0] // 2
    rows = half // chips
    group_rows = half // groups
    mesh_id = pl.DeviceIdType.MESH
    barrier = pltpu.get_barrier_semaphore()

    def peer_chip(step):
        return lax.rem(chip + step, chips)

    def greet(step, carry):
        pl.semaphore_signal(
            barrier, inc=1, device_id=(2 * peer_chip(step) + core,), device_id_type=mesh_id
        )
        return carry

    pl.semaphore_signal(barrier, inc=1, device_id=(partner,), device_id_type=mesh_id)
    lax.fori_loop(1, chips, greet, 0)
    pl.semaphore_wait(barrier, chips)

    def half_at(which, first, size):
        return pl.ds(pl.multiple_of(which * half + first, 16), size)

    def piece(which):
        return pl.ds(pl.multiple_of(which * rows, 16), rows)

    def swap(group):
        return pltpu.make_async_remote_copy(
            src_ref=grads.at[half_at(1 - core, group * group_rows, group_rows)],
            dst_ref=near.at[pl.ds(group * group_rows, group_rows)],
            send_sem=pair_send.at[group],
            recv_sem=pair_recv.at[group],
            device_id=(partner,),
            device_id_type=mesh_id,
        )

    def scatter(target, source):
        return pltpu.make_async_remote_copy(
            src_ref=pair.at[piece(target)],
            dst_ref=landed.at[source],
            send_sem=far_send.at[target],
            recv_sem=far_recv.at[source],
            device_id=(2 * target + core,),
            device_id_type=mesh_id,
        )

    def spread(target, source):
        return pltpu.make_async_remote_copy(
            src_ref=share,
            dst_ref=result.at[half_at(core, source * rows, rows)],
            send_sem=back_send.at[target],
            recv_sem=back_recv.at[source],
            device_id=(2 * target + core,),
            device_id_type=mesh_id,
        )

    def hop(source, which):
        return pltpu.make_async_remote_copy(
            src_ref=result.at[half_at(core, source * rows, rows)],
            dst_ref=result.at[half_at(which, source * rows, rows)],
            send_sem=hop_send.at[source],
            recv_sem=hop_recv.at[source],
            device_id=(partner,),
            device_id_type=mesh_id,
        )

    for group in range(groups):
        swap(group).start()
    per_group = chips // groups
    for group in range(groups):
        swap(group).wait_recv()
        at = pl.ds(group * group_rows, group_rows)
        own = grads[half_at(core, group * group_rows, group_rows), :]
        pair[at, :] = (own.astype(F32) + near[at, :].astype(F32)).astype(BF)
        for place in range(per_group):
            target = group * per_group + place

            @pl.when(target != chip)
            def _(target=target):
                scatter(target, chip).start()

    for group in range(groups):
        swap(group).wait_send()
    landed[chip] = pair[piece(chip), :]

    def arrive(step, carry):
        scatter(peer_chip(step), peer_chip(step)).wait_recv()
        scatter(peer_chip(step), chip).wait_send()
        return carry

    lax.fori_loop(1, chips, arrive, 0)
    total = landed[0].astype(F32)
    for source in range(1, chips):
        total += landed[source].astype(F32)
    final = (total * factor).astype(BF)
    share[...] = final
    result[half_at(core, chip * rows, rows), :] = final

    def send_share(step, carry):
        spread(peer_chip(step), chip).start()
        return carry

    lax.fori_loop(1, chips, send_share, 0)
    hop(chip, core).start()

    def forward(step, carry):
        source = lax.rem(chip + chips - step, chips)
        spread(source, source).wait_recv()
        hop(source, core).start()
        return carry

    lax.fori_loop(1, chips, forward, 0)

    def drain(step, carry):
        hop(step, 1 - core).wait_recv()
        hop(step, core).wait_send()
        return carry

    lax.fori_loop(0, chips, drain, 0)

    def drain_share(step, carry):
        spread(peer_chip(step), chip).wait_send()
        return carry

    lax.fori_loop(1, chips, drain_share, 0)


def memory_kernel(
    devices,
    slots,
    chunk,
    inbox,
    memory,
    edge_weight,
    time_message,
    input_weight,
    hidden_weight,
    gate_bias,
    out_memory,
    out_table,
    picked,
    picked_meta,
    totals,
    counts,
    wide,
):
    rows = memory.shape[0]
    columns = memory.shape[1]
    stride = columns // LANES
    turn = (
        lax.broadcasted_iota(jnp.int32, (slots, LANES), 0)
        == lax.broadcasted_iota(jnp.int32, (slots, LANES), 1)
    ).astype(F32).astype(BF)

    def pick(step, carry):
        for part in range(4):
            source = step * 4 + part
            at = pl.ds(pl.multiple_of(source * slots, slots), slots)
            picked[at, :] = inbox[source, :slots, :]
            picked_meta[at, :] = mm_nt(turn, inbox[source, slots:, :])
        return carry

    lax.fori_loop(0, devices // 4, pick, 0)
    totals[...] = jnp.zeros_like(totals)
    counts[...] = jnp.zeros_like(counts)
    high, low = halves(time_message[...])
    weight = edge_weight[...]

    def add(step, carry):
        at = pl.ds(pl.multiple_of(step * chunk, chunk), chunk)
        info = picked_meta[at, :]
        node, bucket, valid = info[:, 0:1], info[:, 1:2], info[:, 2:3]
        lanes = lax.broadcasted_iota(jnp.int32, (chunk, high.shape[0]), 1).astype(F32)
        picks = (lanes == bucket).astype(F32).astype(BF)
        pre = mm(picked[at, :], weight) + mm(picks, high) + mm(picks, low)
        message = (pre / (1.0 + jnp.exp(-pre))).astype(BF)
        ids = lax.broadcasted_iota(jnp.int32, (chunk, rows), 1).astype(F32)
        hot = jnp.where(ids == node, valid, 0.0).astype(BF)
        totals[...] += mm_tn(hot, message)
        counts[...] += mm_tn(hot, jnp.ones((chunk, LANES), BF))
        return carry

    lax.fori_loop(0, devices * slots // chunk, add, 0)
    count = counts[:, 0:1]
    aggregate = (totals[...] / jnp.maximum(count, 1.0)).astype(BF)
    previous = memory[...]

    def gate(which):
        cut = slice(which * columns, (which + 1) * columns)
        return (
            mm(aggregate, input_weight[:, cut]) + gate_bias[:, cut],
            mm(previous, hidden_weight[:, cut]),
        )

    from_input, from_hidden = gate(0)
    update = jax.nn.sigmoid(from_input + from_hidden)
    from_input, from_hidden = gate(1)
    resets = jax.nn.sigmoid(from_input + from_hidden)
    from_input, from_hidden = gate(2)
    candidate = jnp.tanh(from_input + resets * from_hidden)
    old = previous.astype(F32)
    fresh = (1.0 - update) * candidate + update * old
    fresh = jnp.where(count > 0, fresh, old)
    out_memory[...] = fresh.astype(BF)
    for part in range(stride):
        wide[pl.ds(part, rows, stride=stride), :] = fresh[:, part * LANES : (part + 1) * LANES]
    out_table[...] = wide[...].astype(BF)


def event_kernel(
    resident,
    events,
    fanout,
    ids,
    source,
    buckets,
    affinity,
    upstream,
    time_key,
    query_weight,
    key_weight,
    value_weight,
    out_weight,
    embedding,
    grads,
    *scratch,
):
    columns = upstream.shape[1]
    head = columns // HEADS
    stride = columns // LANES
    if resident:
        landing, table, near, sems, *scratch = scratch
        parts = sems.shape[0]
        size = landing.shape[0] // parts
        copies = []
        for part in range(parts):
            at = pl.ds(part * size, size)
            copies.append(pltpu.make_async_copy(source.at[at], landing.at[at], sems.at[part]))
            copies[-1].start()
    else:
        near = source
        (*scratch,) = scratch
    target, query, back, pull, mix, hits, tq = scratch
    heads = [slice(h * head, (h + 1) * head) for h in range(HEADS)]
    high, low = halves(time_key[...])

    back[...] = mm_nt(upstream[...], out_weight[...]).astype(BF)
    for h, cut in enumerate(heads):
        pull[HEADS + h] = mm_nt(back[:, cut], value_weight[:, cut])

    if resident:
        step_rows = 256
        for part in range(parts):
            copies[part].wait()

            def widen(step, carry, part=part):
                at = pl.ds(pl.multiple_of(part * size + step * step_rows, step_rows), step_rows)
                table[at, :] = landing[at, :].astype(F32)
                return carry

            lax.fori_loop(0, size // step_rows, widen, 0)

        unroll = 16

        def fetch(step, carry):
            for lane in range(unroll):
                row = step * unroll + lane
                start = pl.multiple_of(ids[row], stride)
                near[pl.ds(pl.multiple_of(row * stride, stride), stride), :] = table[
                    pl.ds(start, stride), :
                ]
            return carry

        lax.fori_loop(0, (fanout + 1) * events // unroll, fetch, 0)

    for part in range(stride):
        target[:, part * LANES : (part + 1) * LANES] = near[
            pl.ds(fanout * events * stride + part, events, stride=stride), :
        ].astype(BF)
    query[...] = mm(target[...], query_weight[...]).astype(BF)
    for h, cut in enumerate(heads):
        pull[h] = mm_nt(query[:, cut], key_weight[:, cut])
        tq[h] = mm_nt(query[:, cut], high[:, cut]) + mm_nt(query[:, cut], low[:, cut])

    size = 32
    scale = 1.0 / math.sqrt(head)
    lane = lax.broadcasted_iota(jnp.int32, (size, LANES), 1)
    masks = [(lane >= h * GROUP) & (lane < h * GROUP + fanout) for h in range(HEADS)]

    def per_head(values, op, fill):
        out = jnp.zeros((size, LANES), F32)
        for mask in masks:
            out = jnp.where(
                mask, op(jnp.where(mask, values, fill), axis=1, keepdims=True), out
            )
        return out

    def block(step, carry):
        first = pl.multiple_of(step * size, size)
        at = pl.ds(first, size)
        names = buckets[at, :]

        def rows_of(j, part):
            return near[pl.ds((j * events + first) * stride + part, size, stride=stride), :]

        raw = jnp.zeros((size, LANES), F32)
        for j in range(fanout):
            same = lane == names[:, j : j + 1]
            nearby = [rows_of(j, part) for part in range(stride)]
            for k in range(2 * HEADS):
                total = nearby[0] * pull[k, at, 0:LANES]
                for part in range(1, stride):
                    total += nearby[part] * pull[k, at, part * LANES : (part + 1) * LANES]
                if k < HEADS:
                    total += jnp.where(same, tq[k, at, :], 0.0)
                raw = jnp.where(
                    lane == k * GROUP + j, jnp.sum(total, axis=1, keepdims=True), raw
                )
        scores = raw * scale + affinity[at, :]
        active = masks[0]
        for mask in masks[1:]:
            active = active | mask
        top = per_head(scores, jnp.max, -3.0e38)
        raised = jnp.where(active, jnp.exp(jnp.where(active, scores - top, 0.0)), 0.0)
        below = per_head(raised, jnp.sum, 0.0)
        probs = jnp.where(active, raised / jnp.where(active, below, 1.0), 0.0)
        turned = pltpu.roll(raw, HEADS * GROUP, axis=1).astype(BF).astype(F32)
        slopes = jnp.where(active, turned, 0.0)
        inner = per_head(probs * slopes, jnp.sum, 0.0)
        slopes = probs * (slopes - inner) * scale
        blend = jnp.where(
            active, probs.astype(BF).astype(F32), pltpu.roll(slopes, HEADS * GROUP, axis=1)
        )
        spread = [
            [
                jnp.broadcast_to(blend[:, k * GROUP + j : k * GROUP + j + 1], (size, LANES))
                for j in range(fanout)
            ]
            for k in range(2 * HEADS)
        ]
        for h in range(HEADS):
            total = jnp.zeros((size, LANES), F32)
            for j in range(fanout):
                total += jnp.where(lane == names[:, j : j + 1], spread[HEADS + h][j], 0.0)
            hits[h, at, :] = total.astype(BF)
        for part in range(stride):
            sums = [jnp.zeros((size, LANES), F32) for _ in range(2 * HEADS)]
            for j in range(fanout):
                nearby = rows_of(j, part)
                for k in range(2 * HEADS):
                    sums[k] += spread[k][j] * nearby
            for k in range(2 * HEADS):
                mix[k, at, part * LANES : (part + 1) * LANES] = sums[k].astype(BF)
        return carry

    lax.fori_loop(0, events // size, block, 0)

    for h, cut in enumerate(heads):
        grads[2 * columns : 3 * columns, cut] = mm_tn(mix[h], back[:, cut]).astype(BF)
        grads[columns : 2 * columns, cut] = mm_tn(mix[HEADS + h], query[:, cut]).astype(BF)
    for h, cut in enumerate(heads):
        back[:, cut] = mm(mix[h], value_weight[:, cut]).astype(BF)
        query[:, cut] = (
            mm(mix[HEADS + h], key_weight[:, cut])
            + mm(hits[h], high[:, cut])
            + mm(hits[h], low[:, cut])
        ).astype(BF)
    grads[:columns, :] = mm_tn(target[...], query[...]).astype(BF)
    grads[3 * columns :, :] = mm_tn(back[...], upstream[...]).astype(BF)
    embedding[...] = (mm(back[...], out_weight[...]) + target[...].astype(F32)).astype(BF)


def shards(
    event_node,
    neighbours,
    event_bucket,
    neighbour_bucket,
    edge_features,
    affinity,
    upstream,
    node_memory,
    edge_weight,
    time_message,
    input_weight,
    hidden_weight,
    gate_bias,
    time_key,
    query_weight,
    key_weight,
    value_weight,
    out_weight,
):
    devices = lax.axis_size("node")
    node_rows, columns = node_memory.shape
    events, fanout = neighbours.shape
    features = edge_features.shape[1]
    stride = columns // LANES
    slots = -(-(3 * events // devices) // 16) * 16
    vmem = pl.BlockSpec(memory_space=pltpu.VMEM)
    smem = pl.BlockSpec(memory_space=pltpu.SMEM)

    info = jnp.stack([event_node % node_rows, event_bucket, jnp.ones_like(event_node)])
    info = jnp.pad(info.astype(BF), ((0, 13), (0, 0)))
    owners = (event_node // node_rows).reshape(1, events)
    message_shape = jax.ShapeDtypeStruct((devices, slots + 16, features), BF)
    outgoing = pl.pallas_call(
        functools.partial(pack_kernel, devices, slots),
        out_shape=message_shape,
        in_specs=[vmem] * 3,
        out_specs=vmem,
        scratch_shapes=[pltpu.VMEM((devices, events), F32)],
        name="pack_step",
    )(edge_features, info, owners)
    inbox = pl.pallas_call(
        functools.partial(exchange_kernel, devices),
        out_shape=message_shape,
        in_specs=[vmem],
        out_specs=vmem,
        scratch_shapes=[
            pltpu.SemaphoreType.DMA((devices,)),
            pltpu.SemaphoreType.DMA((devices,)),
            pltpu.SemaphoreType.DMA,
        ],
        compiler_params=pltpu.CompilerParams(collective_id=0, has_side_effects=True),
        name="exchange_step",
    )(outgoing)
    chunk = 256
    new_memory, own_table = pl.pallas_call(
        functools.partial(memory_kernel, devices, slots, chunk),
        out_shape=(
            jax.ShapeDtypeStruct((node_rows, columns), BF),
            jax.ShapeDtypeStruct((node_rows * stride, LANES), BF),
        ),
        in_specs=[vmem] * 7,
        out_specs=(vmem, vmem),
        scratch_shapes=[
            pltpu.VMEM((devices * slots, features), BF),
            pltpu.VMEM((devices * slots, 16), F32),
            pltpu.VMEM((node_rows, columns), F32),
            pltpu.VMEM((node_rows, LANES), F32),
            pltpu.VMEM((node_rows * stride, LANES), F32),
        ],
        compiler_params=pltpu.CompilerParams(vmem_limit_bytes=VMEM_LIMIT),
        name="memory_step",
    )(
        inbox,
        node_memory,
        edge_weight,
        time_message,
        input_weight,
        hidden_weight,
        gate_bias.reshape(1, -1),
    )
    whole = lax.all_gather(own_table, "node", axis=0, tiled=True)

    ids = jnp.concatenate([neighbours.T.reshape(-1), event_node]) * stride
    gap = jnp.zeros((events, GROUP - fanout), F32)
    rest = jnp.zeros((events, LANES - HEADS * GROUP), F32)
    logits = jnp.concatenate([affinity, gap] * HEADS + [rest], axis=1)
    buckets = jnp.pad(neighbour_bucket, ((0, 0), (0, LANES - fanout)))
    resident = whole.size * 4 <= RESIDENT_LIMIT
    near_rows = (fanout + 1) * events * stride
    if resident:
        source = whole
        source_spec = pl.BlockSpec(memory_space=pl.ANY)
        extra = [
            pltpu.VMEM(whole.shape, BF),
            pltpu.VMEM(whole.shape, F32),
            pltpu.VMEM((near_rows, LANES), F32),
            pltpu.SemaphoreType.DMA((8,)),
        ]
    else:
        source = whole.reshape(-1, stride, LANES)[ids // stride]
        source = source.reshape(near_rows, LANES).astype(F32)
        source_spec = vmem
        extra = []
    embedding, grads = pl.pallas_call(
        functools.partial(event_kernel, resident, events, fanout),
        out_shape=(
            jax.ShapeDtypeStruct((events, columns), BF),
            jax.ShapeDtypeStruct((4 * columns, columns), BF),
        ),
        in_specs=[smem, source_spec] + [vmem] * 8,
        out_specs=(vmem, vmem),
        scratch_shapes=extra
        + [
            pltpu.VMEM((events, columns), BF),
            pltpu.VMEM((events, columns), BF),
            pltpu.VMEM((events, columns), BF),
            pltpu.VMEM((2 * HEADS, events, columns), F32),
            pltpu.VMEM((2 * HEADS, events, columns), BF),
            pltpu.VMEM((HEADS, events, LANES), BF),
            pltpu.VMEM((HEADS, events, LANES), F32),
        ],
        compiler_params=pltpu.CompilerParams(vmem_limit_bytes=VMEM_LIMIT),
        name="event_step",
    )(
        ids,
        source,
        buckets,
        logits,
        upstream,
        time_key,
        query_weight,
        key_weight,
        value_weight,
        out_weight,
    )
    chips = devices // 2
    groups = 4
    share = 4 * columns // devices
    factor = 1.0 / math.sqrt(events * devices)
    total = pl.pallas_call(
        functools.partial(reduce_kernel, chips, groups, factor),
        out_shape=jax.ShapeDtypeStruct((4 * columns, columns), BF),
        in_specs=[vmem],
        out_specs=vmem,
        scratch_shapes=[
            pltpu.VMEM((2 * columns, columns), BF),
            pltpu.VMEM((2 * columns, columns), BF),
            pltpu.VMEM((chips, share, columns), BF),
            pltpu.VMEM((share, columns), BF),
            pltpu.SemaphoreType.DMA((groups,)),
            pltpu.SemaphoreType.DMA((groups,)),
        ]
        + [pltpu.SemaphoreType.DMA((chips,)) for _ in range(6)],
        compiler_params=pltpu.CompilerParams(
            collective_id=1, has_side_effects=True, vmem_limit_bytes=VMEM_LIMIT
        ),
        name="reduce_step",
    )(grads).astype(F32)
    return (embedding, new_memory) + tuple(
        total[part * columns : (part + 1) * columns] for part in range(4)
    )


def solution(mesh):
    placed = (
        P("node"),
        P("node", None),
        P("node"),
        P("node", None),
        P("node", None),
        P("node", None),
        P("node", None),
        P("node", None),
        P(),
        P(),
        P(),
        P(),
        P(),
        P(),
        P(),
        P(),
        P(),
        P(),
    )
    return jax.shard_map(
        shards,
        mesh=mesh,
        in_specs=placed,
        out_specs=(P("node", None), P("node", None), P(), P(), P(), P()),
        check_vma=False,
    )
```

```python
import functools
import math

import jax
import jax.numpy as jnp
from jax import lax
from jax.experimental import pallas as pl
from jax.experimental.pallas import tpu as pltpu
from jax.sharding import PartitionSpec as P

HEADS = 2
LANES = 128
GROUP = 32
BF = jnp.bfloat16
F32 = jnp.float32
VMEM_LIMIT = 60 * 1024 * 1024
RESIDENT_LIMIT = 20 * 1024 * 1024
NT = (((1,), (1,)), ((), ()))
TN = (((0,), (0,)), ((), ()))


def mm(a, b):
    return jnp.dot(a, b, preferred_element_type=F32)


def mm_nt(a, b):
    return lax.dot_general(a, b, NT, preferred_element_type=F32)


def mm_tn(a, b):
    return lax.dot_general(a, b, TN, preferred_element_type=F32)


def halves(table):
    high = table.astype(BF)
    low = (table - high.astype(F32)).astype(BF)
    return high, low


def pack_kernel(devices, slots, feats, meta, owners, outgoing, sel):
    events = feats.shape[0]
    ids = lax.broadcasted_iota(jnp.int32, (devices, events), 0)
    theirs = ids == owners[...]
    before = lax.broadcasted_iota(jnp.int32, (events, events), 0) < lax.broadcasted_iota(
        jnp.int32, (events, events), 1
    )
    rank = mm(theirs.astype(F32).astype(BF), before.astype(F32).astype(BF))
    sel[...] = jnp.where(theirs, rank, -1.0)
    slot_ids = lax.broadcasted_iota(jnp.int32, (slots, events), 0).astype(F32)
    lane_ids = lax.broadcasted_iota(jnp.int32, (LANES, events), 0).astype(F32)

    def pick(step, carry):
        for part in range(4):
            device = step * 4 + part
            row = sel[pl.ds(device, 1), :]
            hits = (slot_ids == row).astype(F32).astype(BF)
            outgoing[device, :slots, :] = mm(hits, feats[...]).astype(BF)
            turned = (lane_ids == row).astype(F32).astype(BF)
            outgoing[device, slots:, :] = mm_nt(meta[...], turned).astype(BF)
        return carry

    lax.fori_loop(0, devices // 4, pick, 0)


def exchange_kernel(devices, outgoing, inbox, send_sems, recv_sems, own_sem):
    me = lax.axis_index("node")
    barrier = pltpu.get_barrier_semaphore()

    def greet(step, carry):
        pl.semaphore_signal(
            barrier,
            inc=1,
            device_id=(lax.rem(me + step, devices),),
            device_id_type=pl.DeviceIdType.MESH,
        )
        return carry

    lax.fori_loop(1, devices, greet, 0)
    pl.semaphore_wait(barrier, devices - 1)

    def send(step):
        peer = lax.rem(me + step, devices)
        return pltpu.make_async_remote_copy(
            src_ref=outgoing.at[peer],
            dst_ref=inbox.at[me],
            send_sem=send_sems.at[peer],
            recv_sem=recv_sems.at[me],
            device_id=(peer,),
            device_id_type=pl.DeviceIdType.MESH,
        )

    def receive(step):
        peer = lax.rem(me + step, devices)
        return pltpu.make_async_remote_copy(
            src_ref=outgoing.at[peer],
            dst_ref=inbox.at[peer],
            send_sem=send_sems.at[peer],
            recv_sem=recv_sems.at[peer],
            device_id=(peer,),
            device_id_type=pl.DeviceIdType.MESH,
        )

    def start(step, carry):
        send(step).start()
        return carry

    def finish(step, carry):
        receive(step).wait_recv()
        send(step).wait_send()
        return carry

    lax.fori_loop(1, devices, start, 0)
    own = pltpu.make_async_copy(outgoing.at[me], inbox.at[me], own_sem)
    own.start()
    own.wait()
    lax.fori_loop(1, devices, finish, 0)


def reduce_kernel(
    chips,
    groups,
    factor,
    grads,
    result,
    near,
    pair,
    landed,
    share,
    pair_send,
    pair_recv,
    far_send,
    far_recv,
    back_send,
    back_recv,
    hop_send,
    hop_recv,
):
    me = lax.axis_index("node")
    core = lax.rem(me, 2)
    chip = me // 2
    partner = me + 1 - 2 * core
    half = grads.shape[0] // 2
    rows = half // chips
    group_rows = half // groups
    mesh_id = pl.DeviceIdType.MESH
    barrier = pltpu.get_barrier_semaphore()

    def peer_chip(step):
        return lax.rem(chip + step, chips)

    def greet(step, carry):
        pl.semaphore_signal(
            barrier, inc=1, device_id=(2 * peer_chip(step) + core,), device_id_type=mesh_id
        )
        return carry

    pl.semaphore_signal(barrier, inc=1, device_id=(partner,), device_id_type=mesh_id)
    lax.fori_loop(1, chips, greet, 0)
    pl.semaphore_wait(barrier, chips)

    def half_at(which, first, size):
        return pl.ds(pl.multiple_of(which * half + first, 16), size)

    def piece(which):
        return pl.ds(pl.multiple_of(which * rows, 16), rows)

    def swap(group):
        return pltpu.make_async_remote_copy(
            src_ref=grads.at[half_at(1 - core, group * group_rows, group_rows)],
            dst_ref=near.at[pl.ds(group * group_rows, group_rows)],
            send_sem=pair_send.at[group],
            recv_sem=pair_recv.at[group],
            device_id=(partner,),
            device_id_type=mesh_id,
        )

    def scatter(target, source):
        return pltpu.make_async_remote_copy(
            src_ref=pair.at[piece(target)],
            dst_ref=landed.at[source],
            send_sem=far_send.at[target],
            recv_sem=far_recv.at[source],
            device_id=(2 * target + core,),
            device_id_type=mesh_id,
        )

    def spread(target, source):
        return pltpu.make_async_remote_copy(
            src_ref=share,
            dst_ref=result.at[half_at(core, source * rows, rows)],
            send_sem=back_send.at[target],
            recv_sem=back_recv.at[source],
            device_id=(2 * target + core,),
            device_id_type=mesh_id,
        )

    def hop(source, which):
        return pltpu.make_async_remote_copy(
            src_ref=result.at[half_at(core, source * rows, rows)],
            dst_ref=result.at[half_at(which, source * rows, rows)],
            send_sem=hop_send.at[source],
            recv_sem=hop_recv.at[source],
            device_id=(partner,),
            device_id_type=mesh_id,
        )

    for group in range(groups):
        swap(group).start()
    per_group = chips // groups
    for group in range(groups):
        swap(group).wait_recv()
        at = pl.ds(group * group_rows, group_rows)
        own = grads[half_at(core, group * group_rows, group_rows), :]
        pair[at, :] = (own.astype(F32) + near[at, :].astype(F32)).astype(BF)
        for place in range(per_group):
            target = group * per_group + place

            @pl.when(target != chip)
            def _(target=target):
                scatter(target, chip).start()

    for group in range(groups):
        swap(group).wait_send()
    landed[chip] = pair[piece(chip), :]

    def arrive(step, carry):
        scatter(peer_chip(step), peer_chip(step)).wait_recv()
        scatter(peer_chip(step), chip).wait_send()
        return carry

    lax.fori_loop(1, chips, arrive, 0)
    total = landed[0].astype(F32)
    for source in range(1, chips):
        total += landed[source].astype(F32)
    final = (total * factor).astype(BF)
    share[...] = final
    result[half_at(core, chip * rows, rows), :] = final

    def send_share(step, carry):
        spread(peer_chip(step), chip).start()
        return carry

    lax.fori_loop(1, chips, send_share, 0)
    hop(chip, core).start()

    def forward(step, carry):
        source = lax.rem(chip + chips - step, chips)
        spread(source, source).wait_recv()
        hop(source, core).start()
        return carry

    lax.fori_loop(1, chips, forward, 0)

    def drain(step, carry):
        hop(step, 1 - core).wait_recv()
        hop(step, core).wait_send()
        return carry

    lax.fori_loop(0, chips, drain, 0)

    def drain_share(step, carry):
        spread(peer_chip(step), chip).wait_send()
        return carry

    lax.fori_loop(1, chips, drain_share, 0)


def memory_kernel(
    devices,
    slots,
    chunk,
    inbox,
    memory,
    edge_weight,
    time_message,
    input_weight,
    hidden_weight,
    gate_bias,
    out_memory,
    out_table,
    picked,
    picked_meta,
    totals,
    counts,
    wide,
):
    rows = memory.shape[0]
    columns = memory.shape[1]
    stride = columns // LANES
    turn = (
        lax.broadcasted_iota(jnp.int32, (slots, LANES), 0)
        == lax.broadcasted_iota(jnp.int32, (slots, LANES), 1)
    ).astype(F32).astype(BF)

    def pick(step, carry):
        for part in range(4):
            source = step * 4 + part
            at = pl.ds(pl.multiple_of(source * slots, slots), slots)
            picked[at, :] = inbox[source, :slots, :]
            picked_meta[at, :] = mm_nt(turn, inbox[source, slots:, :])
        return carry

    lax.fori_loop(0, devices // 4, pick, 0)
    totals[...] = jnp.zeros_like(totals)
    counts[...] = jnp.zeros_like(counts)
    high, low = halves(time_message[...])
    weight = edge_weight[...]

    def add(step, carry):
        at = pl.ds(pl.multiple_of(step * chunk, chunk), chunk)
        info = picked_meta[at, :]
        node, bucket, valid = info[:, 0:1], info[:, 1:2], info[:, 2:3]
        lanes = lax.broadcasted_iota(jnp.int32, (chunk, high.shape[0]), 1).astype(F32)
        picks = (lanes == bucket).astype(F32).astype(BF)
        pre = mm(picked[at, :], weight) + mm(picks, high) + mm(picks, low)
        message = (pre / (1.0 + jnp.exp(-pre))).astype(BF)
        ids = lax.broadcasted_iota(jnp.int32, (chunk, rows), 1).astype(F32)
        hot = jnp.where(ids == node, valid, 0.0).astype(BF)
        totals[...] += mm_tn(hot, message)
        counts[...] += mm_tn(hot, jnp.ones((chunk, LANES), BF))
        return carry

    lax.fori_loop(0, devices * slots // chunk, add, 0)
    count = counts[:, 0:1]
    aggregate = (totals[...] / jnp.maximum(count, 1.0)).astype(BF)
    previous = memory[...]

    def gate(which):
        cut = slice(which * columns, (which + 1) * columns)
        return (
            mm(aggregate, input_weight[:, cut]) + gate_bias[:, cut],
            mm(previous, hidden_weight[:, cut]),
        )

    from_input, from_hidden = gate(0)
    update = jax.nn.sigmoid(from_input + from_hidden)
    from_input, from_hidden = gate(1)
    resets = jax.nn.sigmoid(from_input + from_hidden)
    from_input, from_hidden = gate(2)
    candidate = jnp.tanh(from_input + resets * from_hidden)
    old = previous.astype(F32)
    fresh = (1.0 - update) * candidate + update * old
    fresh = jnp.where(count > 0, fresh, old)
    out_memory[...] = fresh.astype(BF)
    for part in range(stride):
        wide[pl.ds(part, rows, stride=stride), :] = fresh[:, part * LANES : (part + 1) * LANES]
    out_table[...] = wide[...].astype(BF)


def gather_kernel(
    line,
    side,
    subs,
    own,
    whole,
    recv,
    hop_recv,
    line_send,
    first_send,
    second_send,
    hop_send,
    own_sem,
):
    me = lax.axis_index("node")
    core = lax.rem(me, 2)
    chip = me // 2
    partner = me + 1 - 2 * core
    low, mid, far = lax.rem(chip, side), lax.rem(chip // side, side), chip // (side * side)
    first = (1 - core) * low + core * mid
    second = (1 - core) * mid + core * low
    first_stride = 1 + core * (side - 1)
    second_stride = side - core * (side - 1)
    rows = own.shape[0]
    size = rows // subs
    mesh_id = pl.DeviceIdType.MESH

    def chip_of(along, over, across):
        return (
            lax.rem(far + line - along, line) * side * side
            + lax.rem(first + side - over, side) * first_stride
            + lax.rem(second + side - across, side) * second_stride
        )

    peers = [2 * chip_of(line - step, 0, 0) + core for step in range(1, line)]
    first_peers = [2 * chip_of(0, side - step, 0) + core for step in range(1, side)]
    second_peers = [2 * chip_of(0, 0, side - step) + core for step in range(1, side)]
    everyone = peers + first_peers + second_peers + [partner]
    barrier = pltpu.get_barrier_semaphore()
    for device in everyone:
        pl.semaphore_signal(barrier, inc=1, device_id=(device,), device_id_type=mesh_id)
    pl.semaphore_wait(barrier, len(everyone))

    def at(source, part, kind):
        return pl.ds(pl.multiple_of((2 * source + kind) * rows + part * size, 16), size)

    def copy(source, part, mine, send_sem, device):
        src = own.at[pl.ds(part * size, size)] if mine else whole.at[at(source, part, core)]
        return pltpu.make_async_remote_copy(
            src_ref=src,
            dst_ref=whole.at[at(source, part, core)],
            send_sem=send_sem,
            recv_sem=recv.at[source * subs + part],
            device_id=(device,),
            device_id_type=mesh_id,
        )

    def hop(source, part, mine, kind):
        src = own.at[pl.ds(part * size, size)] if mine else whole.at[at(source, part, kind)]
        return pltpu.make_async_remote_copy(
            src_ref=src,
            dst_ref=whole.at[at(source, part, kind)],
            send_sem=hop_send.at[source * subs + part],
            recv_sem=hop_recv.at[source * subs + part],
            device_id=(partner,),
            device_id_type=mesh_id,
        )

    started = []

    def start(made):
        made.start()
        started.append(made)

    def landed(source, part):
        copy(source, part, False, hop_send.at[0], partner).wait_recv()

    stay = pltpu.make_async_copy(own, whole.at[pl.ds(pl.multiple_of(me * rows, 16), rows)], own_sem)
    stay.start()
    steps = line * subs
    for step in range(steps + 2):
        if step < steps:
            along, part = divmod(step, subs)
            source = chip_of(along, 0, 0)
            mine = along == 0
            if not mine:
                landed(source, part)
            for to, device in enumerate(first_peers):
                start(copy(source, part, mine, first_send.at[step, to], device))
            if mine:
                for to, device in enumerate(peers):
                    start(copy(source, part, mine, line_send.at[part, to], device))
            for to, device in enumerate(second_peers):
                start(copy(source, part, mine, second_send.at[step, 0, to], device))
            start(hop(source, part, mine, core))
        if 0 <= step - 1 < steps:
            along, part = divmod(step - 1, subs)
            for over in range(1, side):
                source = chip_of(along, over, 0)
                landed(source, part)
                for to, device in enumerate(second_peers):
                    start(copy(source, part, False, second_send.at[step - 1, over, to], device))
                start(hop(source, part, False, core))
        if 0 <= step - 2 < steps:
            along, part = divmod(step - 2, subs)
            for across in range(1, side):
                for over in range(side):
                    source = chip_of(along, over, across)
                    landed(source, part)
                    start(hop(source, part, False, core))
    stay.wait()
    for made in started:
        made.wait_send()

    def drain(source, carry):
        for part in range(subs):
            hop(source, part, False, 1 - core).wait_recv()
        return carry

    lax.fori_loop(0, line * side * side, drain, 0)


def event_kernel(
    resident,
    events,
    fanout,
    ids,
    source,
    buckets,
    affinity,
    upstream,
    time_key,
    query_weight,
    key_weight,
    value_weight,
    out_weight,
    embedding,
    grads,
    *scratch,
):
    columns = upstream.shape[1]
    head = columns // HEADS
    stride = columns // LANES
    if resident:
        landing, table, near, sems, *scratch = scratch
        parts = sems.shape[0]
        size = landing.shape[0] // parts
        copies = []
        for part in range(parts):
            at = pl.ds(part * size, size)
            copies.append(pltpu.make_async_copy(source.at[at], landing.at[at], sems.at[part]))
            copies[-1].start()
    else:
        near = source
        (*scratch,) = scratch
    target, query, back, pull, mix, hits, tq = scratch
    heads = [slice(h * head, (h + 1) * head) for h in range(HEADS)]
    high, low = halves(time_key[...])

    back[...] = mm_nt(upstream[...], out_weight[...]).astype(BF)
    for h, cut in enumerate(heads):
        pull[HEADS + h] = mm_nt(back[:, cut], value_weight[:, cut])

    if resident:
        step_rows = 256
        for part in range(parts):
            copies[part].wait()

            def widen(step, carry, part=part):
                at = pl.ds(pl.multiple_of(part * size + step * step_rows, step_rows), step_rows)
                table[at, :] = landing[at, :].astype(F32)
                return carry

            lax.fori_loop(0, size // step_rows, widen, 0)

        unroll = 16

        def fetch(step, carry):
            for lane in range(unroll):
                row = step * unroll + lane
                start = pl.multiple_of(ids[row], stride)
                near[pl.ds(pl.multiple_of(row * stride, stride), stride), :] = table[
                    pl.ds(start, stride), :
                ]
            return carry

        lax.fori_loop(0, (fanout + 1) * events // unroll, fetch, 0)

    for part in range(stride):
        target[:, part * LANES : (part + 1) * LANES] = near[
            pl.ds(fanout * events * stride + part, events, stride=stride), :
        ].astype(BF)
    query[...] = mm(target[...], query_weight[...]).astype(BF)
    for h, cut in enumerate(heads):
        pull[h] = mm_nt(query[:, cut], key_weight[:, cut])
        tq[h] = mm_nt(query[:, cut], high[:, cut]) + mm_nt(query[:, cut], low[:, cut])

    size = 32
    scale = 1.0 / math.sqrt(head)
    lane = lax.broadcasted_iota(jnp.int32, (size, LANES), 1)
    masks = [(lane >= h * GROUP) & (lane < h * GROUP + fanout) for h in range(HEADS)]

    def per_head(values, op, fill):
        out = jnp.zeros((size, LANES), F32)
        for mask in masks:
            out = jnp.where(
                mask, op(jnp.where(mask, values, fill), axis=1, keepdims=True), out
            )
        return out

    def block(step, carry):
        first = pl.multiple_of(step * size, size)
        at = pl.ds(first, size)
        names = buckets[at, :]

        def rows_of(j, part):
            return near[pl.ds((j * events + first) * stride + part, size, stride=stride), :]

        raw = jnp.zeros((size, LANES), F32)
        for j in range(fanout):
            same = lane == names[:, j : j + 1]
            nearby = [rows_of(j, part) for part in range(stride)]
            for k in range(2 * HEADS):
                total = nearby[0] * pull[k, at, 0:LANES]
                for part in range(1, stride):
                    total += nearby[part] * pull[k, at, part * LANES : (part + 1) * LANES]
                if k < HEADS:
                    total += jnp.where(same, tq[k, at, :], 0.0)
                raw = jnp.where(
                    lane == k * GROUP + j, jnp.sum(total, axis=1, keepdims=True), raw
                )
        scores = raw * scale + affinity[at, :]
        active = masks[0]
        for mask in masks[1:]:
            active = active | mask
        top = per_head(scores, jnp.max, -3.0e38)
        raised = jnp.where(active, jnp.exp(jnp.where(active, scores - top, 0.0)), 0.0)
        below = per_head(raised, jnp.sum, 0.0)
        probs = jnp.where(active, raised / jnp.where(active, below, 1.0), 0.0)
        turned = pltpu.roll(raw, HEADS * GROUP, axis=1).astype(BF).astype(F32)
        slopes = jnp.where(active, turned, 0.0)
        inner = per_head(probs * slopes, jnp.sum, 0.0)
        slopes = probs * (slopes - inner) * scale
        blend = jnp.where(
            active, probs.astype(BF).astype(F32), pltpu.roll(slopes, HEADS * GROUP, axis=1)
        )
        spread = [
            [
                jnp.broadcast_to(blend[:, k * GROUP + j : k * GROUP + j + 1], (size, LANES))
                for j in range(fanout)
            ]
            for k in range(2 * HEADS)
        ]
        for h in range(HEADS):
            total = jnp.zeros((size, LANES), F32)
            for j in range(fanout):
                total += jnp.where(lane == names[:, j : j + 1], spread[HEADS + h][j], 0.0)
            hits[h, at, :] = total.astype(BF)
        for part in range(stride):
            sums = [jnp.zeros((size, LANES), F32) for _ in range(2 * HEADS)]
            for j in range(fanout):
                nearby = rows_of(j, part)
                for k in range(2 * HEADS):
                    sums[k] += spread[k][j] * nearby
            for k in range(2 * HEADS):
                mix[k, at, part * LANES : (part + 1) * LANES] = sums[k].astype(BF)
        return carry

    lax.fori_loop(0, events // size, block, 0)

    for h, cut in enumerate(heads):
        grads[2 * columns : 3 * columns, cut] = mm_tn(mix[h], back[:, cut]).astype(BF)
        grads[columns : 2 * columns, cut] = mm_tn(mix[HEADS + h], query[:, cut]).astype(BF)
    for h, cut in enumerate(heads):
        back[:, cut] = mm(mix[h], value_weight[:, cut]).astype(BF)
        query[:, cut] = (
            mm(mix[HEADS + h], key_weight[:, cut])
            + mm(hits[h], high[:, cut])
            + mm(hits[h], low[:, cut])
        ).astype(BF)
    grads[:columns, :] = mm_tn(target[...], query[...]).astype(BF)
    grads[3 * columns :, :] = mm_tn(back[...], upstream[...]).astype(BF)
    embedding[...] = (mm(back[...], out_weight[...]) + target[...].astype(F32)).astype(BF)


def shards(
    event_node,
    neighbours,
    event_bucket,
    neighbour_bucket,
    edge_features,
    affinity,
    upstream,
    node_memory,
    edge_weight,
    time_message,
    input_weight,
    hidden_weight,
    gate_bias,
    time_key,
    query_weight,
    key_weight,
    value_weight,
    out_weight,
):
    devices = lax.axis_size("node")
    node_rows, columns = node_memory.shape
    events, fanout = neighbours.shape
    features = edge_features.shape[1]
    stride = columns // LANES
    slots = -(-(3 * events // devices) // 16) * 16
    vmem = pl.BlockSpec(memory_space=pltpu.VMEM)
    smem = pl.BlockSpec(memory_space=pltpu.SMEM)

    info = jnp.stack([event_node % node_rows, event_bucket, jnp.ones_like(event_node)])
    info = jnp.pad(info.astype(BF), ((0, 13), (0, 0)))
    owners = (event_node // node_rows).reshape(1, events)
    message_shape = jax.ShapeDtypeStruct((devices, slots + 16, features), BF)
    outgoing = pl.pallas_call(
        functools.partial(pack_kernel, devices, slots),
        out_shape=message_shape,
        in_specs=[vmem] * 3,
        out_specs=vmem,
        scratch_shapes=[pltpu.VMEM((devices, events), F32)],
        name="pack_step",
    )(edge_features, info, owners)
    inbox = pl.pallas_call(
        functools.partial(exchange_kernel, devices),
        out_shape=message_shape,
        in_specs=[vmem],
        out_specs=vmem,
        scratch_shapes=[
            pltpu.SemaphoreType.DMA((devices,)),
            pltpu.SemaphoreType.DMA((devices,)),
            pltpu.SemaphoreType.DMA,
        ],
        compiler_params=pltpu.CompilerParams(collective_id=0, has_side_effects=True),
        name="exchange_step",
    )(outgoing)
    chunk = 256
    new_memory, own_table = pl.pallas_call(
        functools.partial(memory_kernel, devices, slots, chunk),
        out_shape=(
            jax.ShapeDtypeStruct((node_rows, columns), BF),
            jax.ShapeDtypeStruct((node_rows * stride, LANES), BF),
        ),
        in_specs=[vmem] * 7,
        out_specs=(vmem, vmem),
        scratch_shapes=[
            pltpu.VMEM((devices * slots, features), BF),
            pltpu.VMEM((devices * slots, 16), F32),
            pltpu.VMEM((node_rows, columns), F32),
            pltpu.VMEM((node_rows, LANES), F32),
            pltpu.VMEM((node_rows * stride, LANES), F32),
        ],
        compiler_params=pltpu.CompilerParams(vmem_limit_bytes=VMEM_LIMIT),
        name="memory_step",
    )(
        inbox,
        node_memory,
        edge_weight,
        time_message,
        input_weight,
        hidden_weight,
        gate_bias.reshape(1, -1),
    )
    chips = devices // 2
    side = max(s for s in range(1, chips + 1) if chips % (s * s) == 0 and s**3 <= chips)
    line = chips // (side * side)
    subs = 2
    whole = pl.pallas_call(
        functools.partial(gather_kernel, line, side, subs),
        out_shape=jax.ShapeDtypeStruct((devices * node_rows * stride, LANES), BF),
        in_specs=[vmem],
        out_specs=pl.BlockSpec(memory_space=pl.ANY),
        scratch_shapes=[
            pltpu.SemaphoreType.DMA((chips * subs,)),
            pltpu.SemaphoreType.DMA((chips * subs,)),
            pltpu.SemaphoreType.DMA((subs, line - 1)),
            pltpu.SemaphoreType.DMA((line * subs, side - 1)),
            pltpu.SemaphoreType.DMA((line * subs, side, side - 1)),
            pltpu.SemaphoreType.DMA((chips * subs,)),
            pltpu.SemaphoreType.DMA,
        ],
        compiler_params=pltpu.CompilerParams(collective_id=2, has_side_effects=True),
        name="gather_step",
    )(own_table)

    ids = jnp.concatenate([neighbours.T.reshape(-1), event_node]) * stride
    gap = jnp.zeros((events, GROUP - fanout), F32)
    rest = jnp.zeros((events, LANES - HEADS * GROUP), F32)
    logits = jnp.concatenate([affinity, gap] * HEADS + [rest], axis=1)
    buckets = jnp.pad(neighbour_bucket, ((0, 0), (0, LANES - fanout)))
    resident = whole.size * 4 <= RESIDENT_LIMIT
    near_rows = (fanout + 1) * events * stride
    if resident:
        source = whole
        source_spec = pl.BlockSpec(memory_space=pl.ANY)
        extra = [
            pltpu.VMEM(whole.shape, BF),
            pltpu.VMEM(whole.shape, F32),
            pltpu.VMEM((near_rows, LANES), F32),
            pltpu.SemaphoreType.DMA((8,)),
        ]
    else:
        source = whole.reshape(-1, stride, LANES)[ids // stride]
        source = source.reshape(near_rows, LANES).astype(F32)
        source_spec = vmem
        extra = []
    embedding, grads = pl.pallas_call(
        functools.partial(event_kernel, resident, events, fanout),
        out_shape=(
            jax.ShapeDtypeStruct((events, columns), BF),
            jax.ShapeDtypeStruct((4 * columns, columns), BF),
        ),
        in_specs=[smem, source_spec] + [vmem] * 8,
        out_specs=(vmem, vmem),
        scratch_shapes=extra
        + [
            pltpu.VMEM((events, columns), BF),
            pltpu.VMEM((events, columns), BF),
            pltpu.VMEM((events, columns), BF),
            pltpu.VMEM((2 * HEADS, events, columns), F32),
            pltpu.VMEM((2 * HEADS, events, columns), BF),
            pltpu.VMEM((HEADS, events, LANES), BF),
            pltpu.VMEM((HEADS, events, LANES), F32),
        ],
        compiler_params=pltpu.CompilerParams(vmem_limit_bytes=VMEM_LIMIT),
        name="event_step",
    )(
        ids,
        source,
        buckets,
        logits,
        upstream,
        time_key,
        query_weight,
        key_weight,
        value_weight,
        out_weight,
    )
    groups = 4
    share = 4 * columns // devices
    factor = 1.0 / math.sqrt(events * devices)
    total = pl.pallas_call(
        functools.partial(reduce_kernel, chips, groups, factor),
        out_shape=jax.ShapeDtypeStruct((4 * columns, columns), BF),
        in_specs=[vmem],
        out_specs=vmem,
        scratch_shapes=[
            pltpu.VMEM((2 * columns, columns), BF),
            pltpu.VMEM((2 * columns, columns), BF),
            pltpu.VMEM((chips, share, columns), BF),
            pltpu.VMEM((share, columns), BF),
            pltpu.SemaphoreType.DMA((groups,)),
            pltpu.SemaphoreType.DMA((groups,)),
        ]
        + [pltpu.SemaphoreType.DMA((chips,)) for _ in range(6)],
        compiler_params=pltpu.CompilerParams(
            collective_id=1, has_side_effects=True, vmem_limit_bytes=VMEM_LIMIT
        ),
        name="reduce_step",
    )(grads).astype(F32)
    return (embedding, new_memory) + tuple(
        total[part * columns : (part + 1) * columns] for part in range(4)
    )


def solution(mesh):
    placed = (
        P("node"),
        P("node", None),
        P("node"),
        P("node", None),
        P("node", None),
        P("node", None),
        P("node", None),
        P("node", None),
        P(),
        P(),
        P(),
        P(),
        P(),
        P(),
        P(),
        P(),
        P(),
        P(),
    )
    return jax.shard_map(
        shards,
        mesh=mesh,
        in_specs=placed,
        out_specs=(P("node", None), P("node", None), P(), P(), P(), P()),
        check_vma=False,
    )
```
